32 devices in a mesh: path: 8 (over z, x), shard: 4 (over y, core).
Axes of the slice: x: 2, y: 2, z: 4, core: 2. Of those that a mesh axis runs over, the one named last changes fastest.
Arguments:
- master: float32 [2, 4096, 2048], P(None, ('path', 'shard')), may hold values from -6 to 6
- momentum: float32 [2, 4096, 2048], P(None, ('path', 'shard')), may hold values from -2 to 2
- routes: int32 [8, 1], replicated, may hold values from 0 to 1
- counts: int32 [8], replicated, may hold values from 1 to 8
- tokens: bfloat16 [12288, 4096], P(('path', 'shard')), may hold values from -6 to 6
- cotangent: bfloat16 [12288, 2048], P(('path', 'shard')), may hold values from -6 to 6
Outputs:
- master_new: float32 [2, 4096, 2048], P(None, ('path', 'shard'))
- momentum_new: float32 [2, 4096, 2048], P(None, ('path', 'shard'))
The draws below stay inside these ranges and needn't reach their ends.
Inputs may be any that keep to these rules, and one draw needn't show every extreme that they name: `routes`: every module is read by at least one path.
All inputs are finite; a program needn't handle non-finite values.
Results may differ from the reference program's by a relative error of at most 0.0032.
Values may be sent and summed in bfloat16 or wider, within the bound.
No kernel may reach another device: no remote copies, remote signals or barrier semaphores. Data moves between devices by JAX's collectives and lax.ppermute only.
A program may use at most 128 MiB of HBM per device.

```python
import jax
import jax.numpy as jnp
from jax import lax

D = 4096
F = 2048
TOK_DEV = 384
MODULES = 2
TOKENS = 12288
N_PATH = 8
N_SHARD = 4


def set_ends(array, own_key, least, largest):
    spot = [jax.random.randint(jax.random.fold_in(own_key, axis), (), 0, length) for axis, length in enumerate(array.shape)]
    widest = array.shape.index(max(array.shape))
    next_to = spot[:widest] + [(spot[widest] + 1) % array.shape[widest]] + spot[widest + 1:]
    return array.at[tuple(spot)].set(least).at[tuple(next_to)].set(largest)


def level_of(own_key, extent, shards, smallest, top_value):
    loudness = 1.0
    for position, shards_of in shards:
        heights = jax.random.uniform(jax.random.fold_in(jax.random.fold_in(own_key, 6), position), (shards_of,), jnp.float32, smallest / len(shards), top_value / len(shards))
        loudness = loudness * jnp.repeat(jnp.exp(heights), extent[position] // shards_of).reshape((-1,) + (1,) * (len(extent) - 1 - position))
    return loudness


def different_ones(own_key, rows, number_of, top, lift):
    order = jax.random.permutation(jax.random.fold_in(own_key, 1), number_of)
    favour = order
    for power in range(3):
        favour = favour * favour // number_of
    favour = favour * lift // number_of
    chance = jax.random.randint(jax.random.fold_in(own_key, 2), (rows, number_of), 0, 4096) + favour
    sure = jax.random.permutation(jax.random.fold_in(own_key, 3), rows)[jnp.arange(number_of) % rows]
    chance = jnp.where(jnp.arange(rows)[:, None] == sure[None, :], 1 << 14, chance)
    merit = chance * number_of + jnp.arange(number_of)
    return lax.top_k(merit.astype(jnp.int32), top)[1].astype(jnp.int32)


def scatter_about(stream_key, dims, scale, limit, split=(), dtype=jnp.bfloat16):
    factor_of = level_of(stream_key, dims, split, -0.22, 0.18) if split else 1.0
    drawn = jax.random.normal(stream_key, dims, jnp.float32) * scale * factor_of
    return jnp.minimum(jnp.maximum(drawn, -limit), limit).astype(dtype)


def setup_inputs(seed: int = 0) -> dict:
    arg_keys = jax.random.split(jax.random.key(seed), 7)
    return {
        "master": scatter_about(arg_keys[0], (MODULES, D, F), 1.0, 6.0, ((1, 32),), jnp.float32),
        "momentum": scatter_about(arg_keys[1], (MODULES, D, F), 0.3, 2.0, ((1, 32),), jnp.float32),
        "routes": different_ones(arg_keys[2], N_PATH, MODULES, 1, 8192),
        "counts": set_ends(jax.random.randint(arg_keys[3], (N_PATH,), 1, 9), jax.random.fold_in(arg_keys[3], 1), 1, 8).astype(jnp.int32),
        "tokens": scatter_about(arg_keys[4], (TOKENS, D), 1.0, 6.0, ((0, 32),)),
        "cotangent": scatter_about(arg_keys[5], (TOKENS, F), 1.0, 6.0, ((0, 32),)),
    }


def reference(master, momentum, routes, counts, tokens, cotangent):
    inv_root = D ** -0.5
    group_rows = N_SHARD * TOK_DEV
    chosen = routes[:, 0].astype(jnp.int32)
    path_tokens = tokens.reshape(N_PATH, group_rows, D)
    path_cotan = cotangent.reshape(N_PATH, group_rows, F)

    def path_step(running, path_item):
        module_id, weight_count, inputs, cotan = path_item
        weight = master[module_id].astype(jnp.bfloat16)
        pre_act = jnp.dot(inputs, weight, preferred_element_type=jnp.float32) * inv_root
        gate_value = jax.nn.sigmoid(pre_act)
        signal = (cotan.astype(jnp.float32) * gate_value * (1.0 + pre_act * (1.0 - gate_value))).astype(jnp.bfloat16)
        gradient = (jnp.dot(inputs.T, signal, preferred_element_type=jnp.float32) * inv_root).astype(jnp.bfloat16)
        summed = running[0].at[module_id].add(weight_count.astype(jnp.float32) * gradient.astype(jnp.float32))
        totals = running[1].at[module_id].add(weight_count.astype(jnp.float32))
        return (summed, totals), 0

    start_sum = jnp.zeros(master.shape, jnp.float32)
    start_tot = jnp.zeros((master.shape[0],), jnp.float32)
    (summed, totals), unused = lax.scan(path_step, (start_sum, start_tot), (chosen, counts, path_tokens, path_cotan))
    outer_grad = summed / totals[:, None, None]
    momentum_new = 0.9 * momentum + outer_grad
    master_new = master - 0.7 * (outer_grad + 0.9 * momentum_new)
    return master_new, momentum_new
```

```python
import jax
import jax.numpy as jnp
from jax import lax
from jax.experimental import pallas as pl
from jax.experimental.pallas import tpu as pltpu
from jax.sharding import PartitionSpec as P

CHUNKS = 2


def plain(master, momentum, routes, counts, tokens, cotangent):
    path_count = routes.shape[0]
    shards = lax.axis_size("shard")
    modules = master.shape[0]
    rows_block = master.shape[1]
    feat_width = master.shape[2]
    tok_rows = tokens.shape[0]
    model_width = tokens.shape[1]
    inv_root = model_width ** (-0.5)
    chosen = routes[:, 0]
    onehot = (chosen[None, :] == jnp.arange(modules, dtype=jnp.int32)[:, None]).astype(jnp.float32)
    outgoing = jnp.take(master.astype(jnp.bfloat16), chosen, axis=0)
    local_rows = lax.all_to_all(outgoing, "path", split_axis=0, concat_axis=0, tiled=True)
    local_weight = local_rows.reshape(path_count * rows_block, feat_width)
    permuted = tokens.reshape(tok_rows, path_count, shards, rows_block)
    permuted = permuted.transpose(0, 2, 1, 3).reshape(tok_rows, model_width)
    columns = lax.all_to_all(permuted, "shard", split_axis=1, concat_axis=0, tiled=True)
    pre_sum = jnp.dot(
        permuted,
        lax.all_gather(local_weight, "shard", axis=0, tiled=True),
        preferred_element_type=jnp.float32,
    )
    pre_act = pre_sum * inv_root
    gate_value = jax.nn.sigmoid(pre_act)
    signal = (
        cotangent.astype(jnp.float32) * gate_value * (1.0 + pre_act * (1.0 - gate_value))
    ).astype(jnp.bfloat16)
    product = lax.dot_general(
        columns,
        lax.all_gather(signal, "shard", axis=0, tiled=True),
        (((0,), (0,)), ((), ())),
        preferred_element_type=jnp.float32,
    )
    path_grad = (
        (product * inv_root).astype(jnp.bfloat16).reshape(path_count, rows_block, feat_width)
    )
    received = lax.all_to_all(path_grad, "path", split_axis=0, concat_axis=0, tiled=True)
    mixing = onehot * counts.astype(jnp.float32)[None, :]
    mixing = mixing / jnp.sum(mixing, axis=1, keepdims=True)
    flat_recv = received.reshape(path_count, rows_block * feat_width).astype(jnp.float32)
    outer_grad = jnp.dot(mixing, flat_recv, precision=lax.Precision.HIGHEST).reshape(
        modules, rows_block, feat_width
    )
    momentum_new = 0.9 * momentum + outer_grad
    master_new = master - 0.7 * (outer_grad + 0.9 * momentum_new)
    return (master_new, momentum_new)


def column_blocks(tokens, order, width):
    rows = tokens.shape[0]
    sets, blocks = order.shape

    def body(order_ref, src, dst):
        dst[...] = src[...]

    return pl.pallas_call(
        body,
        out_shape=jax.ShapeDtypeStruct((sets, rows, blocks * width), tokens.dtype),
        grid_spec=pltpu.PrefetchScalarGridSpec(
            num_scalar_prefetch=1,
            grid=(sets, blocks),
            in_specs=[pl.BlockSpec((rows, width), lambda a, q, o: (0, o[a, q]))],
            out_specs=pl.BlockSpec((None, rows, width), lambda a, q, o: (a, 0, q)),
        ),
    )(order, tokens)


def ringed(master, momentum, routes, counts, tokens, cotangent):
    bf16, f32 = jnp.bfloat16, jnp.float32
    paths = routes.shape[0]
    modules, rows, feats = master.shape
    tok_rows, model_width = tokens.shape
    inv_root = model_width ** (-0.5)
    ring = paths // 2
    half = feats // 2
    width = half // CHUNKS
    pair = 2 * rows
    p = lax.axis_index("path")
    s = lax.axis_index("shard")
    z, x = p // 2, p % 2
    y, c = s // 2, s % 2
    first = c == 0

    def over(axis, pairs):
        return lambda a: lax.ppermute(a, axis, pairs)

    swap_core = over("shard", [(i, i ^ 1) for i in range(4)])
    swap_y = over("shard", [(i, i ^ 2) for i in range(4)])
    swap_x = over("path", [(i, i ^ 1) for i in range(paths)])
    ahead = over("path", [(i, (i + 2) % paths) for i in range(paths)])
    back = over("path", [(i, (i - 2) % paths) for i in range(paths)])

    def mine_and_other(a):
        low, high = a[..., :half], a[..., half:]
        return jnp.where(first, low, high), jnp.where(first, high, low)

    chosen = routes[:, 0]
    m_own = lax.dynamic_index_in_dim(chosen, p, 0, keepdims=False)
    m_near = lax.dynamic_index_in_dim(chosen, p ^ 1, 0, keepdims=False)
    weight = counts.astype(f32)
    mixing = (chosen[None, :] == jnp.arange(modules, dtype=jnp.int32)[:, None]).astype(f32) * weight[None, :]
    mixing = mixing / jnp.sum(mixing, axis=1, keepdims=True)
    mix_own = lax.dynamic_slice_in_dim(mixing, p, 1, 1).reshape(modules, 1, 1)
    mix_near = lax.dynamic_slice_in_dim(mixing, p ^ 1, 1, 1).reshape(modules, 1, 1)

    keep, give = mine_and_other(master)
    keep, give = keep.astype(bf16), give.astype(bf16)
    got = swap_core(give)
    block = jnp.concatenate(
        [jnp.where(first, keep, got), jnp.where(first, got, keep)], axis=1
    )

    steps = jnp.arange(ring, dtype=jnp.int32)
    owner = ((z - steps) % ring)[:, None] * 2 + (x ^ jnp.arange(2, dtype=jnp.int32))[None, :]
    owner = owner.reshape(-1)
    order = jnp.stack([owner * 2 + (1 - y), owner * 2 + y]).astype(jnp.int32)
    cut = column_blocks(tokens, order, pair)
    tok_far = swap_y(cut[0])
    tok_near = swap_core(cut[1])
    tok_far_near = swap_core(tok_far)
    tok = jnp.concatenate([cut[1], tok_near, tok_far, tok_far_near], axis=0)

    cot_keep, cot_give = mine_and_other(cotangent)
    cot = jnp.concatenate([cot_keep, swap_core(cot_give)], axis=0)

    def gather(j):
        cur = block[:, :, j * width : (j + 1) * width]
        parts = []
        for k in range(ring):
            if k:
                cur = ahead(cur)
            parts.append(lax.dynamic_index_in_dim(cur, m_own, 0, keepdims=False))
            parts.append(swap_x(lax.dynamic_index_in_dim(cur, m_near, 0, keepdims=False)))
        return jnp.concatenate(parts, axis=0)

    near_rows = 2 * tok_rows

    def signals(j, w):
        far = jnp.dot(tok[near_rows:], w, preferred_element_type=f32).astype(bf16)
        far = swap_y(far)
        pre = jnp.dot(tok[:near_rows], w, preferred_element_type=f32)
        pre = (pre + far.astype(f32)) * inv_root
        gate = jax.nn.sigmoid(pre)
        sig = cot[:, j * width : (j + 1) * width].astype(f32) * gate * (1.0 + pre * (1.0 - gate))
        sig = sig.astype(bf16)
        return jnp.concatenate([sig, swap_y(sig)], axis=0)

    def scatter(j, sig):
        grad = lax.dot_general(tok, sig, (((0,), (0,)), ((), ())), preferred_element_type=f32)
        grad = (grad * inv_root).astype(bf16).reshape(ring, 2, pair, width)
        total = None
        for k in reversed(range(ring)):
            near = swap_x(grad[k, 1])
            part = mix_own * grad[k, 0].astype(f32) + mix_near * near.astype(f32)
            if total is not None:
                part = part + total.astype(f32)
            if k:
                total = back(part.astype(bf16))
        low, high = part[:, :rows], part[:, rows:]
        return jnp.where(first, low, high), swap_core(jnp.where(first, high, low))

    kept, came = [], []
    for j in range(CHUNKS):
        a, b = scatter(j, signals(j, gather(j)))
        kept.append(a)
        came.append(b)
    kept, came = jnp.concatenate(kept, axis=2), jnp.concatenate(came, axis=2)
    outer_grad = jnp.concatenate(
        [jnp.where(first, kept, came), jnp.where(first, came, kept)], axis=2
    )
    momentum_new = 0.9 * momentum + outer_grad
    master_new = master - 0.7 * (outer_grad + 0.9 * momentum_new)
    return (master_new, momentum_new)


def solution(mesh):
    placed = (
        P(None, ("path", "shard"), None),
        P(None, ("path", "shard"), None),
        P(),
        P(),
        P(("path", "shard"), None),
        P(("path", "shard"), None),
    )

    def local(master, *rest):
        few = mesh.shape["path"] == 8 and mesh.shape["shard"] == 4 and master.shape[0] <= 2
        return (ringed if few else plain)(master, *rest)

    return jax.shard_map(
        local,
        mesh=mesh,
        in_specs=placed,
        out_specs=(P(None, ("path", "shard"), None), P(None, ("path", "shard"), None)),
        check_vma=False,
    )
```

```python
import jax
import jax.numpy as jnp
from jax import lax
from jax.experimental import pallas as pl
from jax.experimental.pallas import tpu as pltpu
from jax.sharding import PartitionSpec as P

CHUNKS = 4
GATHER_GROUPS = ((0, 1, 2), (3,))
SCATTER_GROUPS = ((3,), (0, 1, 2))
ORDER = (
    "wp", "ws", "cut", "bl", "yt", "z0.1", "ct", "cp", "cc", "tn", "co", "z1.1", "z0.2", "z1.2", "z2.1",
    "x0.0", "z0.3", "z1.3", "x1.0", "z2.2", "z3.1", "cf", "x0.1", "tf", "tk", "w0", "p0", "yp0", "x1.1",
    "x2.0", "z2.3", "w1", "p1", "yp1", "z3.2", "s0", "ys0", "x2.1", "s1", "ys1", "z3.3", "w2", "p2", "yp2",
    "x3.0", "gn0", "go0", "gx0.0", "x3.1", "gx0.1", "gn1", "gx1.0", "gx1.1", "go1", "a0.3", "r0.3", "w3",
    "p3", "yp3", "s2", "ys2", "a0.2", "r0.2", "a1.3", "r1.3", "s3", "ys3", "a0.1", "r0.1", "go2", "gn2",
    "gx2.0", "a1.2", "r1.2", "gx2.1", "a2.3", "r2.3", "a0.0", "fs0", "gn3", "gx3.0", "go3", "gx3.1", "a1.1",
    "r1.1", "a3.3", "r3.3", "a2.2", "r2.2", "a1.0", "fs1", "a3.2", "r3.2", "a2.1", "r2.1", "a3.1", "r3.1",
    "a2.0", "fs2", "a3.0", "fs3", "fin",
)


def plain(master, momentum, routes, counts, tokens, cotangent):
    path_count = routes.shape[0]
    shards = lax.axis_size("shard")
    modules = master.shape[0]
    rows_block = master.shape[1]
    feat_width = master.shape[2]
    tok_rows = tokens.shape[0]
    model_width = tokens.shape[1]
    inv_root = model_width ** (-0.5)
    chosen = routes[:, 0]
    onehot = (chosen[None, :] == jnp.arange(modules, dtype=jnp.int32)[:, None]).astype(jnp.float32)
    outgoing = jnp.take(master.astype(jnp.bfloat16), chosen, axis=0)
    local_rows = lax.all_to_all(outgoing, "path", split_axis=0, concat_axis=0, tiled=True)
    local_weight = local_rows.reshape(path_count * rows_block, feat_width)
    permuted = tokens.reshape(tok_rows, path_count, shards, rows_block)
    permuted = permuted.transpose(0, 2, 1, 3).reshape(tok_rows, model_width)
    columns = lax.all_to_all(permuted, "shard", split_axis=1, concat_axis=0, tiled=True)
    pre_sum = jnp.dot(
        permuted,
        lax.all_gather(local_weight, "shard", axis=0, tiled=True),
        preferred_element_type=jnp.float32,
    )
    pre_act = pre_sum * inv_root
    gate_value = jax.nn.sigmoid(pre_act)
    signal = (
        cotangent.astype(jnp.float32) * gate_value * (1.0 + pre_act * (1.0 - gate_value))
    ).astype(jnp.bfloat16)
    product = lax.dot_general(
        columns,
        lax.all_gather(signal, "shard", axis=0, tiled=True),
        (((0,), (0,)), ((), ())),
        preferred_element_type=jnp.float32,
    )
    path_grad = (
        (product * inv_root).astype(jnp.bfloat16).reshape(path_count, rows_block, feat_width)
    )
    received = lax.all_to_all(path_grad, "path", split_axis=0, concat_axis=0, tiled=True)
    mixing = onehot * counts.astype(jnp.float32)[None, :]
    mixing = mixing / jnp.sum(mixing, axis=1, keepdims=True)
    flat_recv = received.reshape(path_count, rows_block * feat_width).astype(jnp.float32)
    outer_grad = jnp.dot(mixing, flat_recv, precision=lax.Precision.HIGHEST).reshape(
        modules, rows_block, feat_width
    )
    momentum_new = 0.9 * momentum + outer_grad
    master_new = master - 0.7 * (outer_grad + 0.9 * momentum_new)
    return (master_new, momentum_new)


def column_blocks(tokens, places, width):
    rows, columns = tokens.shape
    blocks = places.shape[0] // 2
    tile = rows // 4

    def body(places_ref, src, one, two):
        for q in range(blocks):
            for at, dst in ((q, one), (blocks + q, two)):
                start = pl.multiple_of(places_ref[at] * width, width)
                dst[:, q * width : (q + 1) * width] = src[:, pl.ds(start, width)]

    shape = jax.ShapeDtypeStruct((rows, blocks * width), tokens.dtype)
    return pl.pallas_call(
        body,
        out_shape=(shape, shape),
        grid_spec=pltpu.PrefetchScalarGridSpec(
            num_scalar_prefetch=1,
            grid=(4,),
            in_specs=[pl.BlockSpec((tile, columns), lambda i, o: (i, 0))],
            out_specs=[pl.BlockSpec((tile, blocks * width), lambda i, o: (i, 0))] * 2,
        ),
    )(places, tokens)


def ringed(master, momentum, routes, counts, tokens, cotangent):
    bf16, f32 = jnp.bfloat16, jnp.float32
    paths = routes.shape[0]
    modules, rows, feats = master.shape
    tok_rows, model_width = tokens.shape
    inv_root = model_width ** (-0.5)
    ring = paths // 2
    half = feats // 2
    width = half // CHUNKS
    pair = 2 * rows
    own_rows = ring * pair
    p = lax.axis_index("path")
    s = lax.axis_index("shard")
    z, x = p // 2, p % 2
    y, c = s // 2, s % 2
    first = c == 0

    def over(axis, pairs):
        return lambda a: lax.ppermute(a, axis, pairs)

    swap_core = over("shard", [(i, i ^ 1) for i in range(4)])
    swap_y = over("shard", [(i, i ^ 2) for i in range(4)])
    swap_x = over("path", [(i, i ^ 1) for i in range(paths)])
    ahead = over("path", [(i, (i + 2) % paths) for i in range(paths)])
    back = over("path", [(i, (i - 2) % paths) for i in range(paths)])

    def mine_and_other(a):
        low, high = a[..., :half], a[..., half:]
        return jnp.where(first, low, high), jnp.where(first, high, low)

    chosen = routes[:, 0]
    m_own = lax.dynamic_index_in_dim(chosen, p, 0, keepdims=False)
    m_near = lax.dynamic_index_in_dim(chosen, p ^ 1, 0, keepdims=False)
    weight = counts.astype(f32)
    mixing = (chosen[None, :] == jnp.arange(modules, dtype=jnp.int32)[:, None]).astype(f32) * weight[None, :]
    mixing = mixing / jnp.sum(mixing, axis=1, keepdims=True)
    mix_own = lax.dynamic_slice_in_dim(mixing, p, 1, 1).reshape(modules, 1, 1)
    mix_near = lax.dynamic_slice_in_dim(mixing, p ^ 1, 1, 1).reshape(modules, 1, 1)

    steps = jnp.arange(ring, dtype=jnp.int32)
    owner = jnp.concatenate([((z - steps) % ring) * 2 + x, ((z - steps) % ring) * 2 + (1 - x)])
    places = jnp.concatenate([owner * 2 + (1 - y), owner * 2 + y]).astype(jnp.int32)

    val = {}
    last = [None]

    def after(*values):
        if last[0] is None:
            return values
        return lax.optimization_barrier((*values, last[0]))[:-1]

    def compute(name, fn, *values):
        out = fn(*after(*values))
        val[name] = out
        last[0] = out[0] if isinstance(out, tuple) else out

    def send(name, via, value):
        (value,) = after(value)
        val[name] = via(value)
        last[0] = value

    def stack(*parts):
        return jnp.concatenate(parts, axis=0)

    def start_weights(a):
        keep, give = mine_and_other(a)
        return keep.astype(bf16), give.astype(bf16)

    def full_block(keep, got):
        return jnp.concatenate([jnp.where(first, keep, got), jnp.where(first, got, keep)], axis=1)

    def block_at(j, k):
        return val["bl"][:, :, j * width : (j + 1) * width] if k == 0 else val[f"z{j}.{k}"]

    def pick(m):
        def fn(*blocks):
            return stack(*[lax.dynamic_index_in_dim(b, m, 0, keepdims=False) for b in blocks])

        return fn

    def gathered(j):
        near = [val[f"x{j}.{g}"] for g in range(len(GATHER_GROUPS))]
        return stack(*[pick(m_own)(block_at(j, k)) for k in range(ring)], *near)

    def far_sums(w):
        return jnp.dot(val["tf"], w, preferred_element_type=f32).astype(bf16)

    def signal(j):
        def fn(far):
            pre = jnp.dot(val["tn"], val[f"w{j}"], preferred_element_type=f32)
            pre = (pre + far.astype(f32)) * inv_root
            gate = jax.nn.sigmoid(pre)
            cot = val["co"][:, j * width : (j + 1) * width].astype(f32)
            return (cot * gate * (1.0 + pre * (1.0 - gate))).astype(bf16)

        return fn

    def grad(j, lo):
        def fn(far):
            sig = stack(val[f"s{j}"], far)
            out = lax.dot_general(
                val["tk"][:, lo : lo + own_rows], sig, (((0,), (0,)), ((), ())), preferred_element_type=f32
            )
            return (out * inv_root).astype(bf16)

        return fn

    def piece(j, k):
        for g, group in enumerate(SCATTER_GROUPS):
            if k in group:
                at = group.index(k) * pair
                return val[f"gx{j}.{g}"][at : at + pair]

    def summed(j, k):
        def fn(near, *total):
            part = mix_own * val[f"go{j}"][k * pair : (k + 1) * pair].astype(f32) + mix_near * near.astype(f32)
            if total:
                part = part + total[0].astype(f32)
            if k:
                return part.astype(bf16)
            low, high = part[:, :rows], part[:, rows:]
            return jnp.where(first, high, low), jnp.where(first, low, high)

        return fn

    def task(name):
        kind = name.rstrip("0123456789.")
        number = name[len(kind) :].split(".")
        j = int(number[0]) if number[0] else 0
        k = int(number[1]) if len(number) > 1 else 0
        if kind == "wp":
            compute(name, start_weights, master)
        elif kind == "ws":
            send(name, swap_core, val["wp"][1])
        elif kind == "bl":
            compute(name, full_block, val["wp"][0], val["ws"])
        elif kind == "cut":
            compute(name, lambda t: column_blocks(t, places, pair), tokens)
        elif kind == "yt":
            send(name, swap_y, val["cut"][0])
        elif kind == "ct":
            send(name, swap_core, val["cut"][1])
        elif kind == "cf":
            send(name, swap_core, val["yt"])
        elif kind == "tn":
            compute(name, stack, val["cut"][1], val["ct"])
        elif kind == "tf":
            compute(name, stack, val["yt"], val["cf"])
        elif kind == "tk":
            compute(name, stack, val["tn"], val["tf"])
        elif kind == "cp":
            compute(name, mine_and_other, cotangent)
        elif kind == "cc":
            send(name, swap_core, val["cp"][1])
        elif kind == "co":
            compute(name, stack, val["cp"][0], val["cc"])
        elif kind == "z":
            send(name, ahead, block_at(j, k - 1))
        elif kind == "x":
            compute(name, pick(m_near), *[block_at(j, i) for i in GATHER_GROUPS[k]])
            send(name, swap_x, val[name])
        elif kind == "w":
            val[name] = gathered(j)
        elif kind == "p":
            compute(name, far_sums, val[f"w{j}"])
        elif kind == "yp":
            send(name, swap_y, val[f"p{j}"])
        elif kind == "s":
            compute(name, signal(j), val[f"yp{j}"])
        elif kind == "ys":
            send(name, swap_y, val[f"s{j}"])
        elif kind == "gn":
            compute(name, grad(j, own_rows), val[f"ys{j}"])
        elif kind == "go":
            compute(name, grad(j, 0), val[f"ys{j}"])
        elif kind == "gx":
            group = SCATTER_GROUPS[k]
            send(name, swap_x, val[f"gn{j}"][group[0] * pair : (group[-1] + 1) * pair])
        elif kind == "a":
            compute(name, summed(j, k), piece(j, k), *([val[f"r{j}.{k + 1}"]] if k < ring - 1 else []))
        elif kind == "r":
            send(name, back, val[f"a{j}.{k}"])
        elif kind == "fs":
            send(name, swap_core, val[f"a{j}.0"][0])

    for name in ORDER:
        task(name)
    kept = jnp.concatenate([val[f"a{j}.0"][1] for j in range(CHUNKS)], axis=2)
    came = jnp.concatenate([val[f"fs{j}"] for j in range(CHUNKS)], axis=2)
    outer_grad = jnp.concatenate(
        [jnp.where(first, kept, came), jnp.where(first, came, kept)], axis=2
    )
    momentum_new = 0.9 * momentum + outer_grad
    master_new = master - 0.7 * (outer_grad + 0.9 * momentum_new)
    return (master_new, momentum_new)


def solution(mesh):
    placed = (
        P(None, ("path", "shard"), None),
        P(None, ("path", "shard"), None),
        P(),
        P(),
        P(("path", "shard"), None),
        P(("path", "shard"), None),
    )

    def local(master, *rest):
        few = mesh.shape["path"] == 8 and mesh.shape["shard"] == 4 and master.shape[0] <= 2
        return (ringed if few else plain)(master, *rest)

    return jax.shard_map(
        local,
        mesh=mesh,
        in_specs=placed,
        out_specs=(P(None, ("path", "shard"), None), P(None, ("path", "shard"), None)),
        check_vma=False,
    )
```

```python
import jax
import jax.numpy as jnp
from jax import lax
from jax.experimental import pallas as pl
from jax.experimental.pallas import tpu as pltpu
from jax.sharding import PartitionSpec as P

CHUNKS = (2, 2, 2, 2)
GATHER_GROUPS = ((0, 1, 2), (3,))
SCATTER_GROUPS = ((3,), (0, 1, 2))
TOKEN_PARTS = 1
ORDER = (
    "wp", "ws", "cut", "bl", "ya0", "z0.1", "ct", "z1.1", "cp", "rt", "z0.2", "cc", "z1.2", "tn", "co",
    "z2.1", "x0.0", "z0.3", "z1.3", "x1.0", "z2.2", "z3.1", "cf0", "x0.1", "tf", "tk", "w0", "p0", "yp0",
    "x1.1", "x2.0", "z2.3", "w1", "p1", "yp1", "z3.2", "s0", "ys0", "x2.1", "s1", "ys1", "z3.3", "w2", "p2",
    "yp2", "x3.0", "gn0", "go0", "gx0.0", "x3.1", "gx0.1", "gn1", "gx1.0", "gx1.1", "go1", "a0.3", "r0.3",
    "w3", "p3", "yp3", "s2", "ys2", "a0.2", "r0.2", "a1.3", "r1.3", "s3", "ys3", "a0.1", "r0.1", "go2",
    "gn2", "gx2.0", "a1.2", "r1.2", "gx2.1", "a2.3", "r2.3", "a0.0", "fs0", "gn3", "gx3.0", "go3", "gx3.1",
    "a1.1", "r1.1", "a3.3", "r3.3", "a2.2", "r2.2", "a1.0", "fs1", "a3.2", "r3.2", "a2.1", "r2.1", "a3.1",
    "r3.1", "a2.0", "fs2", "a3.0", "fs3",
)

def plain(master, momentum, routes, counts, tokens, cotangent):
    path_count = routes.shape[0]
    shards = lax.axis_size("shard")
    modules = master.shape[0]
    rows_block = master.shape[1]
    feat_width = master.shape[2]
    tok_rows = tokens.shape[0]
    model_width = tokens.shape[1]
    inv_root = model_width ** (-0.5)
    chosen = routes[:, 0]
    onehot = (chosen[None, :] == jnp.arange(modules, dtype=jnp.int32)[:, None]).astype(jnp.float32)
    outgoing = jnp.take(master.astype(jnp.bfloat16), chosen, axis=0)
    local_rows = lax.all_to_all(outgoing, "path", split_axis=0, concat_axis=0, tiled=True)
    local_weight = local_rows.reshape(path_count * rows_block, feat_width)
    permuted = tokens.reshape(tok_rows, path_count, shards, rows_block)
    permuted = permuted.transpose(0, 2, 1, 3).reshape(tok_rows, model_width)
    columns = lax.all_to_all(permuted, "shard", split_axis=1, concat_axis=0, tiled=True)
    pre_sum = jnp.dot(
        permuted,
        lax.all_gather(local_weight, "shard", axis=0, tiled=True),
        preferred_element_type=jnp.float32,
    )
    pre_act = pre_sum * inv_root
    gate_value = jax.nn.sigmoid(pre_act)
    signal = (
        cotangent.astype(jnp.float32) * gate_value * (1.0 + pre_act * (1.0 - gate_value))
    ).astype(jnp.bfloat16)
    product = lax.dot_general(
        columns,
        lax.all_gather(signal, "shard", axis=0, tiled=True),
        (((0,), (0,)), ((), ())),
        preferred_element_type=jnp.float32,
    )
    path_grad = (
        (product * inv_root).astype(jnp.bfloat16).reshape(path_count, rows_block, feat_width)
    )
    received = lax.all_to_all(path_grad, "path", split_axis=0, concat_axis=0, tiled=True)
    mixing = onehot * counts.astype(jnp.float32)[None, :]
    mixing = mixing / jnp.sum(mixing, axis=1, keepdims=True)
    flat_recv = received.reshape(path_count, rows_block * feat_width).astype(jnp.float32)
    outer_grad = jnp.dot(mixing, flat_recv, precision=lax.Precision.HIGHEST).reshape(
        modules, rows_block, feat_width
    )
    momentum_new = 0.9 * momentum + outer_grad
    master_new = master - 0.7 * (outer_grad + 0.9 * momentum_new)
    return (master_new, momentum_new)


def column_blocks(tokens, places, width):
    rows, columns = tokens.shape
    blocks = places.shape[0] // 2
    tile = rows // 4

    def body(places_ref, src, one, two):
        for q in range(blocks):
            for at, dst in ((q, one), (blocks + q, two)):
                start = pl.multiple_of(places_ref[at] * width, width)
                dst[:, q * width : (q + 1) * width] = src[:, pl.ds(start, width)]

    shape = jax.ShapeDtypeStruct((rows, blocks * width), tokens.dtype)
    return pl.pallas_call(
        body,
        out_shape=(shape, shape),
        grid_spec=pltpu.PrefetchScalarGridSpec(
            num_scalar_prefetch=1,
            grid=(4,),
            in_specs=[pl.BlockSpec((tile, columns), lambda i, o: (i, 0))],
            out_specs=[pl.BlockSpec((tile, blocks * width), lambda i, o: (i, 0))] * 2,
        ),
    )(places, tokens)


def ringed(master, momentum, routes, counts, tokens, cotangent):
    bf16, f32 = jnp.bfloat16, jnp.float32
    paths = routes.shape[0]
    modules, rows, feats = master.shape
    tok_rows, model_width = tokens.shape
    inv_root = model_width ** (-0.5)
    ring = paths // 2
    half = feats // 2
    widths = [half * part // sum(CHUNKS) for part in CHUNKS]
    starts = [sum(widths[:j]) for j in range(len(widths))]
    pair = 2 * rows
    own_rows = ring * pair
    p = lax.axis_index("path")
    s = lax.axis_index("shard")
    z, x = p // 2, p % 2
    y, c = s // 2, s % 2
    first = c == 0

    def over(axis, pairs):
        return lambda a: lax.ppermute(a, axis, pairs)

    swap_core = over("shard", [(i, i ^ 1) for i in range(4)])
    swap_y = over("shard", [(i, i ^ 2) for i in range(4)])
    swap_x = over("path", [(i, i ^ 1) for i in range(paths)])
    ahead = over("path", [(i, (i + 2) % paths) for i in range(paths)])
    back = over("path", [(i, (i - 2) % paths) for i in range(paths)])

    def mine_and_other(a):
        low, high = a[..., :half], a[..., half:]
        return jnp.where(first, low, high), jnp.where(first, high, low)

    steps = jnp.arange(ring, dtype=jnp.int32)
    owner = jnp.concatenate([((z - steps) % ring) * 2 + x, ((z - steps) % ring) * 2 + (1 - x)])
    places = jnp.concatenate([owner * 2 + (1 - y), owner * 2 + y]).astype(jnp.int32)
    part_rows = tok_rows // TOKEN_PARTS

    val = {}
    last = [None]

    def after(*values):
        if last[0] is None:
            return values
        return lax.optimization_barrier((*values, last[0]))[: len(values)]

    def compute(name, fn, *values):
        out = fn(*after(*values))
        val[name] = out
        last[0] = out[0] if isinstance(out, tuple) else out

    def send(name, via, value):
        (value,) = after(value)
        val[name] = via(value)
        last[0] = value

    def stack(*parts):
        return jnp.concatenate(parts, axis=0)

    def route_values(routes, counts):
        chosen = routes[:, 0]
        m_own = lax.dynamic_index_in_dim(chosen, p, 0, keepdims=False)
        m_near = lax.dynamic_index_in_dim(chosen, p ^ 1, 0, keepdims=False)
        weight = counts.astype(f32)
        every = jnp.arange(modules, dtype=jnp.int32)
        mixing = (chosen[None, :] == every[:, None]).astype(f32) * weight[None, :]
        mixing = mixing / jnp.sum(mixing, axis=1, keepdims=True)
        mix_own = lax.dynamic_slice_in_dim(mixing, p, 1, 1).reshape(modules, 1, 1)
        mix_near = lax.dynamic_slice_in_dim(mixing, p ^ 1, 1, 1).reshape(modules, 1, 1)
        return m_own, m_near, mix_own, mix_near

    def start_weights(a):
        keep, give = mine_and_other(a)
        return keep.astype(bf16), give.astype(bf16)

    def full_block(keep, got):
        return jnp.concatenate([jnp.where(first, keep, got), jnp.where(first, got, keep)], axis=1)

    def block_at(j, k):
        return val["bl"][:, :, starts[j] : starts[j] + widths[j]] if k == 0 else val[f"z{j}.{k}"]

    def pick(m):
        def fn(*blocks):
            return stack(*[lax.dynamic_index_in_dim(b, m, 0, keepdims=False) for b in blocks])

        return fn

    def gathered(j):
        near = [val[f"x{j}.{g}"] for g in range(len(GATHER_GROUPS))]
        return stack(*[pick(val["rt"][0])(block_at(j, k)) for k in range(ring)], *near)

    def far_sums(w):
        return jnp.dot(val["tf"], w, preferred_element_type=f32).astype(bf16)

    def signal(j):
        def fn(far):
            pre = jnp.dot(val["tn"], val[f"w{j}"], preferred_element_type=f32)
            pre = (pre + far.astype(f32)) * inv_root
            gate = jax.nn.sigmoid(pre)
            cot = val["co"][:, starts[j] : starts[j] + widths[j]].astype(f32)
            return (cot * gate * (1.0 + pre * (1.0 - gate))).astype(bf16)

        return fn

    def grad(j, lo):
        def fn(far):
            sig = stack(val[f"s{j}"], far)
            out = lax.dot_general(
                val["tk"][:, lo : lo + own_rows], sig, (((0,), (0,)), ((), ())), preferred_element_type=f32
            )
            return (out * inv_root).astype(bf16)

        return fn

    def piece(j, k):
        for g, group in enumerate(SCATTER_GROUPS):
            if k in group:
                at = group.index(k) * pair
                return val[f"gx{j}.{g}"][at : at + pair]

    def summed(j, k):
        def fn(near, *total):
            _, _, mix_own, mix_near = val["rt"]
            part = mix_own * val[f"go{j}"][k * pair : (k + 1) * pair].astype(f32) + mix_near * near.astype(f32)
            if total:
                part = part + total[0].astype(f32)
            if k:
                return part.astype(bf16)
            low, high = part[:, :rows], part[:, rows:]
            return jnp.where(first, high, low), jnp.where(first, low, high)

        return fn

    def task(name):
        kind = name.rstrip("0123456789.")
        number = name[len(kind) :].split(".")
        j = int(number[0]) if number[0] else 0
        k = int(number[1]) if len(number) > 1 else 0
        if kind == "wp":
            compute(name, start_weights, master)
        elif kind == "ws":
            send(name, swap_core, val["wp"][1])
        elif kind == "bl":
            compute(name, full_block, val["wp"][0], val["ws"])
        elif kind == "rt":
            compute(name, route_values, routes, counts)
        elif kind == "cut":
            compute(name, lambda t: column_blocks(t, places, pair), tokens)
        elif kind == "ct":
            send(name, swap_core, val["cut"][1])
        elif kind == "ya":
            send(name, swap_y, val["cut"][0][j * part_rows : (j + 1) * part_rows])
        elif kind == "cf":
            send(name, swap_core, val[f"ya{j}"])
        elif kind == "tn":
            compute(name, stack, val["cut"][1], val["ct"])
        elif kind == "tf":
            compute(name, stack, *[val[f"{way}{i}"] for way in ("ya", "cf") for i in range(TOKEN_PARTS)])
        elif kind == "tk":
            compute(name, stack, val["tn"], val["tf"])
        elif kind == "cp":
            compute(name, mine_and_other, cotangent)
        elif kind == "cc":
            send(name, swap_core, val["cp"][1])
        elif kind == "co":
            compute(name, stack, val["cp"][0], val["cc"])
        elif kind == "z":
            send(name, ahead, block_at(j, k - 1))
        elif kind == "x":
            compute(name, pick(val["rt"][1]), *[block_at(j, i) for i in GATHER_GROUPS[k]])
            send(name, swap_x, val[name])
        elif kind == "w":
            val[name] = gathered(j)
        elif kind == "p":
            compute(name, far_sums, val[f"w{j}"])
        elif kind == "yp":
            send(name, swap_y, val[f"p{j}"])
        elif kind == "s":
            compute(name, signal(j), val[f"yp{j}"])
        elif kind == "ys":
            send(name, swap_y, val[f"s{j}"])
        elif kind == "gn":
            compute(name, grad(j, own_rows), val[f"ys{j}"])
        elif kind == "go":
            compute(name, grad(j, 0), val[f"ys{j}"])
        elif kind == "gx":
            group = SCATTER_GROUPS[k]
            send(name, swap_x, val[f"gn{j}"][group[0] * pair : (group[-1] + 1) * pair])
        elif kind == "a":
            compute(name, summed(j, k), piece(j, k), *([val[f"r{j}.{k + 1}"]] if k < ring - 1 else []))
        elif kind == "r":
            send(name, back, val[f"a{j}.{k}"])
        elif kind == "fs":
            send(name, swap_core, val[f"a{j}.0"][0])

    for name in ORDER:
        task(name)
    kept = jnp.concatenate([val[f"a{j}.0"][1] for j in range(len(widths))], axis=2)
    came = jnp.concatenate([val[f"fs{j}"] for j in range(len(widths))], axis=2)
    outer_grad = jnp.concatenate(
        [jnp.where(first, kept, came), jnp.where(first, came, kept)], axis=2
    )
    momentum_new = 0.9 * momentum + outer_grad
    master_new = master - 0.7 * (outer_grad + 0.9 * momentum_new)
    return (master_new, momentum_new)


def solution(mesh):
    placed = (
        P(None, ("path", "shard"), None),
        P(None, ("path", "shard"), None),
        P(),
        P(),
        P(("path", "shard"), None),
        P(("path", "shard"), None),
    )

    def local(master, *rest):
        few = mesh.shape["path"] == 8 and mesh.shape["shard"] == 4 and master.shape[0] <= 2
        return (ringed if few else plain)(master, *rest)

    return jax.shard_map(
        local,
        mesh=mesh,
        in_specs=placed,
        out_specs=(P(None, ("path", "shard"), None), P(None, ("path", "shard"), None)),
        check_vma=False,
    )
```

```python
import jax
import jax.numpy as jnp
from jax import lax
from jax.experimental import pallas as pl
from jax.experimental.pallas import tpu as pltpu
from jax.sharding import PartitionSpec as P

CHUNKS = (2, 2, 2, 2)
GATHER_GROUPS = ((0, 1, 2), (3,))
SCATTER_GROUPS = ((3,), (0, 1, 2))
TOKEN_PARTS = 1
ORDER = (
    "wp", "ws", "cut", "ct", "bl", "ya0", "z0.1", "z1.1", "cp", "rt", "z0.2", "cc", "z1.2", "tn", "co",
    "z2.1", "x0.0", "z0.3", "z1.3", "x1.0", "z2.2", "z3.1", "cf0", "x0.1", "tf", "tk", "w0", "p0", "yp0",
    "x1.1", "x2.0", "z2.3", "w1", "p1", "yp1", "z3.2", "s0", "ys0", "x3.0", "x2.1", "s1", "ys1", "z3.3",
    "w2", "p2", "yp2", "gn0", "go0", "gx0.0", "x3.1", "gx0.1", "gn1", "gx1.0", "gx1.1", "go1", "a0.3",
    "r0.3", "w3", "p3", "yp3", "s2", "ys2", "a0.2", "r0.2", "a1.3", "r1.3", "s3", "ys3", "a0.1", "r0.1",
    "go2", "gn2", "gx2.0", "a1.2", "r1.2", "gx2.1", "a2.3", "r2.3", "a0.0", "fs0", "gn3", "gx3.0", "go3",
    "gx3.1", "a1.1", "r1.1", "a3.3", "r3.3", "a2.2", "r2.2", "a1.0", "fs1", "a3.2", "r3.2", "a2.1", "r2.1",
    "a3.1", "r3.1", "a2.0", "fs2", "a3.0", "fs3", "d:r3.3",
)

def plain(master, momentum, routes, counts, tokens, cotangent):
    path_count = routes.shape[0]
    shards = lax.axis_size("shard")
    modules = master.shape[0]
    rows_block = master.shape[1]
    feat_width = master.shape[2]
    tok_rows = tokens.shape[0]
    model_width = tokens.shape[1]
    inv_root = model_width ** (-0.5)
    chosen = routes[:, 0]
    onehot = (chosen[None, :] == jnp.arange(modules, dtype=jnp.int32)[:, None]).astype(jnp.float32)
    outgoing = jnp.take(master.astype(jnp.bfloat16), chosen, axis=0)
    local_rows = lax.all_to_all(outgoing, "path", split_axis=0, concat_axis=0, tiled=True)
    local_weight = local_rows.reshape(path_count * rows_block, feat_width)
    permuted = tokens.reshape(tok_rows, path_count, shards, rows_block)
    permuted = permuted.transpose(0, 2, 1, 3).reshape(tok_rows, model_width)
    columns = lax.all_to_all(permuted, "shard", split_axis=1, concat_axis=0, tiled=True)
    pre_sum = jnp.dot(
        permuted,
        lax.all_gather(local_weight, "shard", axis=0, tiled=True),
        preferred_element_type=jnp.float32,
    )
    pre_act = pre_sum * inv_root
    gate_value = jax.nn.sigmoid(pre_act)
    signal = (
        cotangent.astype(jnp.float32) * gate_value * (1.0 + pre_act * (1.0 - gate_value))
    ).astype(jnp.bfloat16)
    product = lax.dot_general(
        columns,
        lax.all_gather(signal, "shard", axis=0, tiled=True),
        (((0,), (0,)), ((), ())),
        preferred_element_type=jnp.float32,
    )
    path_grad = (
        (product * inv_root).astype(jnp.bfloat16).reshape(path_count, rows_block, feat_width)
    )
    received = lax.all_to_all(path_grad, "path", split_axis=0, concat_axis=0, tiled=True)
    mixing = onehot * counts.astype(jnp.float32)[None, :]
    mixing = mixing / jnp.sum(mixing, axis=1, keepdims=True)
    flat_recv = received.reshape(path_count, rows_block * feat_width).astype(jnp.float32)
    outer_grad = jnp.dot(mixing, flat_recv, precision=lax.Precision.HIGHEST).reshape(
        modules, rows_block, feat_width
    )
    momentum_new = 0.9 * momentum + outer_grad
    master_new = master - 0.7 * (outer_grad + 0.9 * momentum_new)
    return (master_new, momentum_new)


def column_blocks(tokens, places, width):
    rows, columns = tokens.shape
    blocks = places.shape[0] // 2
    tile = rows // 4

    def body(places_ref, src, one, two):
        for q in range(blocks):
            for at, dst in ((q, one), (blocks + q, two)):
                start = pl.multiple_of(places_ref[at] * width, width)
                dst[:, q * width : (q + 1) * width] = src[:, pl.ds(start, width)]

    shape = jax.ShapeDtypeStruct((rows, blocks * width), tokens.dtype)
    return pl.pallas_call(
        body,
        out_shape=(shape, shape),
        grid_spec=pltpu.PrefetchScalarGridSpec(
            num_scalar_prefetch=1,
            grid=(4,),
            in_specs=[pl.BlockSpec((tile, columns), lambda i, o: (i, 0))],
            out_specs=[pl.BlockSpec((tile, blocks * width), lambda i, o: (i, 0))] * 2,
        ),
    )(places, tokens)


def ringed(master, momentum, routes, counts, tokens, cotangent):
    bf16, f32 = jnp.bfloat16, jnp.float32
    paths = routes.shape[0]
    modules, rows, feats = master.shape
    tok_rows, model_width = tokens.shape
    inv_root = model_width ** (-0.5)
    ring = paths // 2
    half = feats // 2
    widths = [half * part // sum(CHUNKS) for part in CHUNKS]
    starts = [sum(widths[:j]) for j in range(len(widths))]
    pair = 2 * rows
    own_rows = ring * pair
    p = lax.axis_index("path")
    s = lax.axis_index("shard")
    z, x = p // 2, p % 2
    y, c = s // 2, s % 2
    first = c == 0

    def over(axis, pairs):
        return lambda a: lax.ppermute(a, axis, pairs)

    swap_core = over("shard", [(i, i ^ 1) for i in range(4)])
    swap_y = over("shard", [(i, i ^ 2) for i in range(4)])
    swap_x = over("path", [(i, i ^ 1) for i in range(paths)])
    ahead = over("path", [(i, (i + 2) % paths) for i in range(paths)])
    back = over("path", [(i, (i - 2) % paths) for i in range(paths)])

    def mine_and_other(a):
        low, high = a[..., :half], a[..., half:]
        return jnp.where(first, low, high), jnp.where(first, high, low)

    steps = jnp.arange(ring, dtype=jnp.int32)
    owner = jnp.concatenate([((z - steps) % ring) * 2 + x, ((z - steps) % ring) * 2 + (1 - x)])
    places = jnp.concatenate([owner * 2 + (1 - y), owner * 2 + y]).astype(jnp.int32)
    part_rows = tok_rows // TOKEN_PARTS

    val = {}
    last = [None]
    arrived = []

    def after(*values):
        if last[0] is None:
            return values
        held = lax.optimization_barrier((*values, last[0], *arrived))[: len(values)]
        arrived.clear()
        return held

    def compute(name, fn, *values):
        out = fn(*after(*values))
        val[name] = out
        last[0] = out[0] if isinstance(out, tuple) else out

    def send(name, via, value):
        (value,) = after(value)
        val[name] = via(value)
        last[0] = value

    def stack(*parts):
        return jnp.concatenate(parts, axis=0)

    def route_values(routes, counts):
        chosen = routes[:, 0]
        m_own = lax.dynamic_index_in_dim(chosen, p, 0, keepdims=False)
        m_near = lax.dynamic_index_in_dim(chosen, p ^ 1, 0, keepdims=False)
        weight = counts.astype(f32)
        every = jnp.arange(modules, dtype=jnp.int32)
        mixing = (chosen[None, :] == every[:, None]).astype(f32) * weight[None, :]
        mixing = mixing / jnp.sum(mixing, axis=1, keepdims=True)
        mix_own = lax.dynamic_slice_in_dim(mixing, p, 1, 1).reshape(modules, 1, 1)
        mix_near = lax.dynamic_slice_in_dim(mixing, p ^ 1, 1, 1).reshape(modules, 1, 1)
        return m_own, m_near, mix_own, mix_near

    def start_weights(a):
        keep, give = mine_and_other(a)
        return keep.astype(bf16), give.astype(bf16)

    def full_block(keep, got):
        return jnp.concatenate([jnp.where(first, keep, got), jnp.where(first, got, keep)], axis=1)

    def block_at(j, k):
        return val["bl"][:, :, starts[j] : starts[j] + widths[j]] if k == 0 else val[f"z{j}.{k}"]

    def pick(m):
        def fn(*blocks):
            return stack(*[lax.dynamic_index_in_dim(b, m, 0, keepdims=False) for b in blocks])

        return fn

    def gathered(j):
        near = [val[f"x{j}.{g}"] for g in range(len(GATHER_GROUPS))]
        return stack(*[pick(val["rt"][0])(block_at(j, k)) for k in range(ring)], *near)

    def far_sums(w):
        return jnp.dot(val["tf"], w, preferred_element_type=f32).astype(bf16)

    def signal(j):
        def fn(far):
            pre = jnp.dot(val["tn"], val[f"w{j}"], preferred_element_type=f32)
            pre = (pre + far.astype(f32)) * inv_root
            gate = jax.nn.sigmoid(pre)
            cot = val["co"][:, starts[j] : starts[j] + widths[j]].astype(f32)
            return (cot * gate * (1.0 + pre * (1.0 - gate))).astype(bf16)

        return fn

    def grad(j, lo):
        def fn(far):
            sig = stack(val[f"s{j}"], far)
            out = lax.dot_general(
                val["tk"][:, lo : lo + own_rows], sig, (((0,), (0,)), ((), ())), preferred_element_type=f32
            )
            return (out * inv_root).astype(bf16)

        return fn

    def piece(j, k):
        for g, group in enumerate(SCATTER_GROUPS):
            if k in group:
                at = group.index(k) * pair
                return val[f"gx{j}.{g}"][at : at + pair]

    def summed(j, k):
        def fn(near, *total):
            _, _, mix_own, mix_near = val["rt"]
            part = mix_own * val[f"go{j}"][k * pair : (k + 1) * pair].astype(f32) + mix_near * near.astype(f32)
            if total:
                part = part + total[0].astype(f32)
            if k:
                return part.astype(bf16)
            low, high = part[:, :rows], part[:, rows:]
            return jnp.where(first, high, low), jnp.where(first, low, high)

        return fn

    def task(name):
        kind = name.rstrip("0123456789.")
        number = name[len(kind) :].split(".")
        j = int(number[0]) if number[0] else 0
        k = int(number[1]) if len(number) > 1 else 0
        if kind == "wp":
            compute(name, start_weights, master)
        elif kind == "ws":
            send(name, swap_core, val["wp"][1])
        elif kind == "bl":
            compute(name, full_block, val["wp"][0], val["ws"])
        elif kind == "rt":
            compute(name, route_values, routes, counts)
        elif kind == "cut":
            compute(name, lambda t: column_blocks(t, places, pair), tokens)
        elif kind == "ct":
            send(name, swap_core, val["cut"][1])
        elif kind == "ya":
            send(name, swap_y, val["cut"][0][j * part_rows : (j + 1) * part_rows])
        elif kind == "cf":
            send(name, swap_core, val[f"ya{j}"])
        elif kind == "tn":
            compute(name, stack, val["cut"][1], val["ct"])
        elif kind == "tf":
            compute(name, stack, *[val[f"{way}{i}"] for way in ("ya", "cf") for i in range(TOKEN_PARTS)])
        elif kind == "tk":
            compute(name, stack, val["tn"], val["tf"])
        elif kind == "cp":
            compute(name, mine_and_other, cotangent)
        elif kind == "cc":
            send(name, swap_core, val["cp"][1])
        elif kind == "co":
            compute(name, stack, val["cp"][0], val["cc"])
        elif kind == "z":
            send(name, ahead, block_at(j, k - 1))
        elif kind == "x":
            compute(name, pick(val["rt"][1]), *[block_at(j, i) for i in GATHER_GROUPS[k]])
            send(name, swap_x, val[name])
        elif kind == "w":
            val[name] = gathered(j)
        elif kind == "p":
            compute(name, far_sums, val[f"w{j}"])
        elif kind == "yp":
            send(name, swap_y, val[f"p{j}"])
        elif kind == "s":
            compute(name, signal(j), val[f"yp{j}"])
        elif kind == "ys":
            send(name, swap_y, val[f"s{j}"])
        elif kind == "gn":
            compute(name, grad(j, own_rows), val[f"ys{j}"])
        elif kind == "go":
            compute(name, grad(j, 0), val[f"ys{j}"])
        elif kind == "gx":
            group = SCATTER_GROUPS[k]
            send(name, swap_x, val[f"gn{j}"][group[0] * pair : (group[-1] + 1) * pair])
        elif kind == "a":
            compute(name, summed(j, k), piece(j, k), *([val[f"r{j}.{k + 1}"]] if k < ring - 1 else []))
        elif kind == "r":
            send(name, back, val[f"a{j}.{k}"])
        elif kind == "fs":
            send(name, swap_core, val[f"a{j}.0"][0])

    for name in ORDER:
        if name.startswith("d:"):
            arrived.append(val[name[2:]])
        else:
            task(name)
    kept = jnp.concatenate([val[f"a{j}.0"][1] for j in range(len(widths))], axis=2)
    came = jnp.concatenate([val[f"fs{j}"] for j in range(len(widths))], axis=2)
    outer_grad = jnp.concatenate(
        [jnp.where(first, kept, came), jnp.where(first, came, kept)], axis=2
    )
    momentum_new = 0.9 * momentum + outer_grad
    master_new = master - 0.7 * (outer_grad + 0.9 * momentum_new)
    return (master_new, momentum_new)


def solution(mesh):
    placed = (
        P(None, ("path", "shard"), None),
        P(None, ("path", "shard"), None),
        P(),
        P(),
        P(("path", "shard"), None),
        P(("path", "shard"), None),
    )

    def local(master, *rest):
        few = mesh.shape["path"] == 8 and mesh.shape["shard"] == 4 and master.shape[0] <= 2
        return (ringed if few else plain)(master, *rest)

    return jax.shard_map(
        local,
        mesh=mesh,
        in_specs=placed,
        out_specs=(P(None, ("path", "shard"), None), P(None, ("path", "shard"), None)),
        check_vma=False,
    )
```

```python
import jax
import jax.numpy as jnp
from jax import lax
from jax.experimental import pallas as pl
from jax.experimental.pallas import tpu as pltpu
from jax.sharding import PartitionSpec as P

CHUNKS = (2, 2, 2, 2)
GATHER_GROUPS = ((0, 1, 2), (3,))
SCATTER_GROUPS = ((3,), (0, 1, 2))
TOKEN_PARTS = 1
ORDER = (
    "wp", "ws", "cut", "ct", "bl", "ya0", "z0.1", "z1.1", "cp", "rt", "z0.2", "cc", "z1.2", "tn", "co",
    "z2.1", "x0.0", "z0.3", "z1.3", "x1.0", "z2.2", "z3.1", "cf0", "x0.1", "tf", "w0", "p0", "yp0", "tk",
    "x1.1", "x2.0", "z2.3", "w1", "p1", "yp1", "z3.2", "s0", "ys0", "x3.0", "x2.1", "s1", "ys1", "z3.3",
    "w2", "p2", "yp2", "gn0", "go0", "gx0.0", "x3.1", "gx0.1", "gn1", "gx1.0", "gx1.1", "go1", "a0.3",
    "r0.3", "w3", "p3", "yp3", "s2", "ys2", "a0.2", "r0.2", "a1.3", "r1.3", "s3", "ys3", "a0.1", "r0.1",
    "go2", "gn2", "gx2.0", "a1.2", "r1.2", "gx2.1", "a2.3", "r2.3", "a0.0", "fs0", "gn3", "gx3.0", "go3",
    "gx3.1", "a1.1", "r1.1", "a3.3", "r3.3", "a2.2", "r2.2", "a1.0", "fs1", "a3.2", "r3.2", "a2.1", "r2.1",
    "a3.1", "r3.1", "a2.0", "fs2", "a3.0", "fs3",
)

def plain(master, momentum, routes, counts, tokens, cotangent):
    path_count = routes.shape[0]
    shards = lax.axis_size("shard")
    modules = master.shape[0]
    rows_block = master.shape[1]
    feat_width = master.shape[2]
    tok_rows = tokens.shape[0]
    model_width = tokens.shape[1]
    inv_root = model_width ** (-0.5)
    chosen = routes[:, 0]
    onehot = (chosen[None, :] == jnp.arange(modules, dtype=jnp.int32)[:, None]).astype(jnp.float32)
    outgoing = jnp.take(master.astype(jnp.bfloat16), chosen, axis=0)
    local_rows = lax.all_to_all(outgoing, "path", split_axis=0, concat_axis=0, tiled=True)
    local_weight = local_rows.reshape(path_count * rows_block, feat_width)
    permuted = tokens.reshape(tok_rows, path_count, shards, rows_block)
    permuted = permuted.transpose(0, 2, 1, 3).reshape(tok_rows, model_width)
    columns = lax.all_to_all(permuted, "shard", split_axis=1, concat_axis=0, tiled=True)
    pre_sum = jnp.dot(
        permuted,
        lax.all_gather(local_weight, "shard", axis=0, tiled=True),
        preferred_element_type=jnp.float32,
    )
    pre_act = pre_sum * inv_root
    gate_value = jax.nn.sigmoid(pre_act)
    signal = (
        cotangent.astype(jnp.float32) * gate_value * (1.0 + pre_act * (1.0 - gate_value))
    ).astype(jnp.bfloat16)
    product = lax.dot_general(
        columns,
        lax.all_gather(signal, "shard", axis=0, tiled=True),
        (((0,), (0,)), ((), ())),
        preferred_element_type=jnp.float32,
    )
    path_grad = (
        (product * inv_root).astype(jnp.bfloat16).reshape(path_count, rows_block, feat_width)
    )
    received = lax.all_to_all(path_grad, "path", split_axis=0, concat_axis=0, tiled=True)
    mixing = onehot * counts.astype(jnp.float32)[None, :]
    mixing = mixing / jnp.sum(mixing, axis=1, keepdims=True)
    flat_recv = received.reshape(path_count, rows_block * feat_width).astype(jnp.float32)
    outer_grad = jnp.dot(mixing, flat_recv, precision=lax.Precision.HIGHEST).reshape(
        modules, rows_block, feat_width
    )
    momentum_new = 0.9 * momentum + outer_grad
    master_new = master - 0.7 * (outer_grad + 0.9 * momentum_new)
    return (master_new, momentum_new)


def column_blocks(tokens, places, width):
    rows, columns = tokens.shape
    blocks = places.shape[0] // 2
    tile = rows // 4

    def body(places_ref, src, one, two):
        for q in range(blocks):
            for at, dst in ((q, one), (blocks + q, two)):
                start = pl.multiple_of(places_ref[at] * width, width)
                dst[:, q * width : (q + 1) * width] = src[:, pl.ds(start, width)]

    shape = jax.ShapeDtypeStruct((rows, blocks * width), tokens.dtype)
    return pl.pallas_call(
        body,
        out_shape=(shape, shape),
        grid_spec=pltpu.PrefetchScalarGridSpec(
            num_scalar_prefetch=1,
            grid=(4,),
            in_specs=[pl.BlockSpec((tile, columns), lambda i, o: (i, 0))],
            out_specs=[pl.BlockSpec((tile, blocks * width), lambda i, o: (i, 0))] * 2,
        ),
    )(places, tokens)


def ringed(master, momentum, routes, counts, tokens, cotangent):
    bf16, f32 = jnp.bfloat16, jnp.float32
    paths = routes.shape[0]
    modules, rows, feats = master.shape
    tok_rows, model_width = tokens.shape
    inv_root = model_width ** (-0.5)
    ring = paths // 2
    half = feats // 2
    widths = [half * part // sum(CHUNKS) for part in CHUNKS]
    starts = [sum(widths[:j]) for j in range(len(widths))]
    pair = 2 * rows
    own_rows = ring * pair
    p = lax.axis_index("path")
    s = lax.axis_index("shard")
    z, x = p // 2, p % 2
    y, c = s // 2, s % 2
    first = c == 0

    def over(axis, pairs):
        return lambda a: lax.ppermute(a, axis, pairs)

    swap_core = over("shard", [(i, i ^ 1) for i in range(4)])
    swap_y = over("shard", [(i, i ^ 2) for i in range(4)])
    swap_x = over("path", [(i, i ^ 1) for i in range(paths)])
    ahead = over("path", [(i, (i + 2) % paths) for i in range(paths)])
    back = over("path", [(i, (i - 2) % paths) for i in range(paths)])

    def mine_and_other(a):
        low, high = a[..., :half], a[..., half:]
        return jnp.where(first, low, high), jnp.where(first, high, low)

    steps = jnp.arange(ring, dtype=jnp.int32)
    owner = jnp.concatenate([((z - steps) % ring) * 2 + x, ((z - steps) % ring) * 2 + (1 - x)])
    places = jnp.concatenate([owner * 2 + (1 - y), owner * 2 + y]).astype(jnp.int32)
    part_rows = tok_rows // TOKEN_PARTS

    val = {}
    last = [None]
    arrived = []

    def after(*values):
        if last[0] is None:
            return values
        held = lax.optimization_barrier((*values, last[0], *arrived))[: len(values)]
        arrived.clear()
        return held

    def compute(name, fn, *values):
        out = fn(*after(*values))
        val[name] = out
        last[0] = out[0] if isinstance(out, tuple) else out

    def send(name, via, value):
        (value,) = after(value)
        val[name] = via(value)
        last[0] = value

    def stack(*parts):
        return jnp.concatenate(parts, axis=0)

    def route_values(routes, counts):
        chosen = routes[:, 0]
        m_own = lax.dynamic_index_in_dim(chosen, p, 0, keepdims=False)
        m_near = lax.dynamic_index_in_dim(chosen, p ^ 1, 0, keepdims=False)
        weight = counts.astype(f32)
        every = jnp.arange(modules, dtype=jnp.int32)
        mixing = (chosen[None, :] == every[:, None]).astype(f32) * weight[None, :]
        mixing = mixing / jnp.sum(mixing, axis=1, keepdims=True)
        mix_own = lax.dynamic_slice_in_dim(mixing, p, 1, 1).reshape(modules, 1, 1)
        mix_near = lax.dynamic_slice_in_dim(mixing, p ^ 1, 1, 1).reshape(modules, 1, 1)
        return m_own, m_near, mix_own, mix_near

    def start_weights(a):
        keep, give = mine_and_other(a)
        return keep.astype(bf16), give.astype(bf16)

    def full_block(keep, got):
        return jnp.concatenate([jnp.where(first, keep, got), jnp.where(first, got, keep)], axis=1)

    def block_at(j, k):
        return val["bl"][:, :, starts[j] : starts[j] + widths[j]] if k == 0 else val[f"z{j}.{k}"]

    def pick(m):
        def fn(*blocks):
            return stack(*[lax.dynamic_index_in_dim(b, m, 0, keepdims=False) for b in blocks])

        return fn

    def gathered(j):
        near = [val[f"x{j}.{g}"] for g in range(len(GATHER_GROUPS))]
        return stack(*[pick(val["rt"][0])(block_at(j, k)) for k in range(ring)], *near)

    def far_sums(w):
        return jnp.dot(val["tf"], w, preferred_element_type=f32).astype(bf16)

    def signal(j):
        def fn(far):
            pre = jnp.dot(val["tn"], val[f"w{j}"], preferred_element_type=f32)
            pre = (pre + far.astype(f32)) * inv_root
            gate = jax.nn.sigmoid(pre)
            cot = val["co"][:, starts[j] : starts[j] + widths[j]].astype(f32)
            return (cot * gate * (1.0 + pre * (1.0 - gate))).astype(bf16)

        return fn

    def grad(j, lo):
        def fn(far):
            sig = stack(val[f"s{j}"], far)
            out = lax.dot_general(
                val["tk"][:, lo : lo + own_rows], sig, (((0,), (0,)), ((), ())), preferred_element_type=f32
            )
            return (out * inv_root).astype(bf16)

        return fn

    def piece(j, k):
        for g, group in enumerate(SCATTER_GROUPS):
            if k in group:
                at = group.index(k) * pair
                return val[f"gx{j}.{g}"][at : at + pair]

    def summed(j, k):
        def fn(near, *total):
            _, _, mix_own, mix_near = val["rt"]
            part = mix_own * val[f"go{j}"][k * pair : (k + 1) * pair].astype(f32) + mix_near * near.astype(f32)
            if total:
                part = part + total[0].astype(f32)
            if k:
                return part.astype(bf16)
            low, high = part[:, :rows], part[:, rows:]
            return jnp.where(first, high, low), jnp.where(first, low, high)

        return fn

    def task(name):
        kind = name.rstrip("0123456789.")
        number = name[len(kind) :].split(".")
        j = int(number[0]) if number[0] else 0
        k = int(number[1]) if len(number) > 1 else 0
        if kind == "wp":
            compute(name, start_weights, master)
        elif kind == "ws":
            send(name, swap_core, val["wp"][1])
        elif kind == "bl":
            compute(name, full_block, val["wp"][0], val["ws"])
        elif kind == "rt":
            compute(name, route_values, routes, counts)
        elif kind == "cut":
            compute(name, lambda t: column_blocks(t, places, pair), tokens)
        elif kind == "ct":
            send(name, swap_core, val["cut"][1])
        elif kind == "ya":
            send(name, swap_y, val["cut"][0][j * part_rows : (j + 1) * part_rows])
        elif kind == "cf":
            send(name, swap_core, val[f"ya{j}"])
        elif kind == "tn":
            compute(name, stack, val["cut"][1], val["ct"])
        elif kind == "tf":
            compute(name, stack, *[val[f"{way}{i}"] for way in ("ya", "cf") for i in range(TOKEN_PARTS)])
        elif kind == "tk":
            compute(name, stack, val["tn"], val["tf"])
        elif kind == "cp":
            compute(name, mine_and_other, cotangent)
        elif kind == "cc":
            send(name, swap_core, val["cp"][1])
        elif kind == "co":
            compute(name, stack, val["cp"][0], val["cc"])
        elif kind == "z":
            send(name, ahead, block_at(j, k - 1))
        elif kind == "x":
            compute(name, pick(val["rt"][1]), *[block_at(j, i) for i in GATHER_GROUPS[k]])
            send(name, swap_x, val[name])
        elif kind == "w":
            val[name] = gathered(j)
        elif kind == "p":
            compute(name, far_sums, val[f"w{j}"])
        elif kind == "yp":
            send(name, swap_y, val[f"p{j}"])
        elif kind == "s":
            compute(name, signal(j), val[f"yp{j}"])
        elif kind == "ys":
            send(name, swap_y, val[f"s{j}"])
        elif kind == "gn":
            compute(name, grad(j, own_rows), val[f"ys{j}"])
        elif kind == "go":
            compute(name, grad(j, 0), val[f"ys{j}"])
        elif kind == "gx":
            group = SCATTER_GROUPS[k]
            send(name, swap_x, val[f"gn{j}"][group[0] * pair : (group[-1] + 1) * pair])
        elif kind == "a":
            compute(name, summed(j, k), piece(j, k), *([val[f"r{j}.{k + 1}"]] if k < ring - 1 else []))
        elif kind == "r":
            send(name, back, val[f"a{j}.{k}"])
        elif kind == "fs":
            send(name, swap_core, val[f"a{j}.0"][0])

    for name in ORDER:
        if name.startswith("d:"):
            arrived.append(val[name[2:]])
        else:
            task(name)
    kept = jnp.concatenate([val[f"a{j}.0"][1] for j in range(len(widths))], axis=2)
    came = jnp.concatenate([val[f"fs{j}"] for j in range(len(widths))], axis=2)
    outer_grad = jnp.concatenate(
        [jnp.where(first, kept, came), jnp.where(first, came, kept)], axis=2
    )
    momentum_new = 0.9 * momentum + outer_grad
    master_new = master - 0.7 * (outer_grad + 0.9 * momentum_new)
    return (master_new, momentum_new)


def solution(mesh):
    placed = (
        P(None, ("path", "shard"), None),
        P(None, ("path", "shard"), None),
        P(),
        P(),
        P(("path", "shard"), None),
        P(("path", "shard"), None),
    )

    def local(master, *rest):
        few = mesh.shape["path"] == 8 and mesh.shape["shard"] == 4 and master.shape[0] <= 2
        return (ringed if few else plain)(master, *rest)

    return jax.shard_map(
        local,
        mesh=mesh,
        in_specs=placed,
        out_specs=(P(None, ("path", "shard"), None), P(None, ("path", "shard"), None)),
        check_vma=False,
    )
```
